256 devices in a mesh: pw: 64 (over x_lo, z, y), band: 4 (over x_hi, core).
Axes of the slice: x: 4 (x_hi: 2, x_lo: 2; x = x_hi * 2 + x_lo), y: 4, z: 8, core: 2. Of those that a mesh axis runs over, the one named last changes fastest.
Arguments:
- residual_directions: float32 [2, 512, 4, 16384], P(None, 'pw', 'band'), may hold values from -6 to 6
- local_field_applied: float32 [2, 512, 4, 16384], P(None, 'pw', 'band'), may hold values from -6 to 6
- orbital_running_sum: bfloat16 [2, 2048, 4, 16384], P(None, None, 'band', 'pw'), may hold values from -6 to 6
- energy_operator_running_sum: bfloat16 [2, 2048, 4, 16384], P(None, None, 'band', 'pw'), may hold values from -6 to 6
- coefficient_store: bfloat16 [4, 512, 2048], P('band'), may hold values from -0.25 to 0.25
- slab_keepers: int32 [2], replicated, may hold values from 0 to 3
- lattice_position: int32 [4, 16384], P('band', 'pw'), may hold values from 0 to 262143
Outputs:
- psi_new: bfloat16 [2, 2048, 4, 16384], P(None, None, 'band', 'pw')
- hpsi_new: bfloat16 [2, 2048, 4, 16384], P(None, None, 'band', 'pw')
The draws below stay inside these ranges and needn't reach their ends.
Inputs may be any that keep to these rules, and one draw needn't show every extreme that they name: `slab_keepers`: each panel's owner is an index along band. `lattice_position`: grid points are row-major indices of a 64 x 64 x 64 grid, not necessarily distinct.
All inputs are finite; a program needn't handle non-finite values.
Results may differ from the reference program's by a relative error of at most 0.001.
Values may be sent and summed in bfloat16 or wider, within the bound.
No kernel may reach another device: no remote copies, remote signals or barrier semaphores. Data moves between devices by JAX's collectives and lax.ppermute only.
A program may use at most 128 MiB of HBM per device.

```python
import jax
import jax.numpy as jnp
from jax import lax

RESIDUAL_NUMBER = 512
SLAB_LENGTH = 256
ORBITAL_SPAN = 2048
GRID = 64
PANELS = 2
PWG = 16384
N_BAND = 4


def with_ends(result, own_key, low, high):
    spot = [jax.random.randint(jax.random.fold_in(own_key, axis), (), 0, length) for axis, length in enumerate(result.shape)]
    longest = result.shape.index(max(result.shape))
    beside = spot[:longest] + [(spot[longest] + 1) % result.shape[longest]] + spot[longest + 1:]
    return result.at[tuple(spot)].set(low).at[tuple(beside)].set(high)


def steps_of(key, dims, shards, smallest, top_value):
    gain, own = 1.0, jax.random.fold_in(key, 6)
    for dim, blocks in shards:
        heights = jnp.exp(jax.random.uniform(jax.random.fold_in(own, dim), (blocks,), jnp.float32, smallest / len(shards), top_value / len(shards)))
        gain = gain * jnp.repeat(heights, dims[dim] // blocks).reshape([-1 if axis == dim else 1 for axis in range(len(dims))])
    return gain


def noise(own_key, dims, deviation, bound, shards=(), held_as=jnp.bfloat16):
    level = steps_of(own_key, dims, shards, -0.22, 0.18) if shards else 1.0
    array = jax.random.normal(own_key, dims, jnp.float32) * deviation * level
    return jnp.minimum(jnp.maximum(array, -bound), bound).astype(held_as)


def setup_inputs(seed: int = 0) -> dict:
    streams_of = jax.random.split(jax.random.key(seed), 8)
    return {
        "residual_directions": noise(streams_of[0], (2, RESIDUAL_NUMBER, N_BAND, PWG), 1.0, 6.0, ((1, 64), (2, 4)), jnp.float32),
        "local_field_applied": noise(streams_of[1], (2, RESIDUAL_NUMBER, N_BAND, PWG), 1.0, 6.0, ((1, 64), (2, 4)), jnp.float32),
        "orbital_running_sum": noise(streams_of[2], (2, ORBITAL_SPAN, N_BAND, PWG), 1.0, 6.0, ((2, 4), (3, 64))),
        "energy_operator_running_sum": noise(streams_of[3], (2, ORBITAL_SPAN, N_BAND, PWG), 1.0, 6.0, ((2, 4), (3, 64))),
        "coefficient_store": noise(streams_of[4], (N_BAND, RESIDUAL_NUMBER, ORBITAL_SPAN), RESIDUAL_NUMBER ** -0.5, 0.25, ((0, 4),)),
        "slab_keepers": jax.random.randint(streams_of[5], (PANELS,), 0, N_BAND).astype(jnp.int32),
        "lattice_position": with_ends(jax.random.randint(streams_of[6], (N_BAND, PWG), 0, GRID ** 3), jax.random.fold_in(streams_of[6], 1), 0, (GRID ** 3) - 1).astype(jnp.int32),
    }


def kinetic_of(lattice_position):
    first = lattice_position // (GRID * GRID)
    second = (lattice_position // GRID) % GRID
    third = lattice_position % GRID
    total = jnp.zeros(lattice_position.shape, jnp.int32)
    for index in (first, second, third):
        folded = jnp.where(index >= GRID // 2, index - GRID, index)
        total = total + folded * folded
    return total.astype(jnp.float32) / (GRID * GRID)


def reference(residual_directions, local_field_applied, orbital_running_sum, energy_operator_running_sum, coefficient_store, slab_keepers, lattice_position):
    kinetic = kinetic_of(lattice_position)
    hcorr = kinetic[None, None, :, :] * residual_directions + local_field_applied
    selected_rows = []
    for subspace_slab in range(RESIDUAL_NUMBER // SLAB_LENGTH):
        keeper_processor = slab_keepers[subspace_slab].astype(jnp.int32)
        line_segment = lax.dynamic_index_in_dim(coefficient_store, keeper_processor, 0, keepdims=False)
        selected_rows.append(line_segment[subspace_slab * SLAB_LENGTH:(subspace_slab + 1) * SLAB_LENGTH])
    eigenvector_matrix = jnp.concatenate(selected_rows, axis=0).astype(jnp.float32)

    def one_group(items):
        corr_b, hcorr_b, psi_b, hpsi_b = items
        stacked_vectors = jnp.concatenate([corr_b, hcorr_b], axis=0)
        rotation_product = jnp.einsum("tu,gtm->gum", eigenvector_matrix, stacked_vectors, precision=lax.Precision.HIGHEST)
        psi_out = (psi_b.astype(jnp.float32) + rotation_product[:2]).astype(jnp.bfloat16)
        hpsi_out = (hpsi_b.astype(jnp.float32) + rotation_product[2:]).astype(jnp.bfloat16)
        return psi_out, hpsi_out

    psi_blocks, hpsi_blocks = lax.map(one_group, (jnp.moveaxis(residual_directions, 2, 0), jnp.moveaxis(hcorr, 2, 0), jnp.moveaxis(orbital_running_sum, 2, 0), jnp.moveaxis(energy_operator_running_sum, 2, 0)))
    return jnp.moveaxis(psi_blocks, 0, 2), jnp.moveaxis(hpsi_blocks, 0, 2)
```

```python
import functools

import jax
import jax.numpy as jnp
from jax import lax
from jax.experimental import pallas as pl
from jax.experimental.pallas import tpu as pltpu
from jax.sharding import PartitionSpec as P

GRID = 64
LANES = 128
ROWS = 16
STEPS = 256.0
TOP = 32600.0


def pack_body(r_ref, l_ref, out_ref):
    dests = out_ref.shape[0]
    stride = 2 * dests
    sources = [ref.reshape(ROWS * stride, LANES) for ref in (r_ref, l_ref)]
    lane = lax.broadcasted_iota(jnp.int32, (8, LANES), 1)
    for d in range(dests):
        codes = []
        for a, ref in enumerate(sources):
            halves = [ref[pl.ds(2 * d + p, ROWS, stride=stride), :] for p in range(2)]
            top = jnp.maximum(jnp.abs(halves[0]), jnp.abs(halves[1]))
            top = jnp.max(top, axis=1, keepdims=True)
            code = jnp.ceil(jnp.log2(jnp.maximum(top, 1e-30)) * STEPS) + 1.0
            inverse = jnp.exp2(code * (-1.0 / STEPS)) * TOP
            for p in range(2):
                q = jnp.round(halves[p] * inverse).astype(jnp.int32)
                at = p * 2 * ROWS + a * ROWS
                out_ref[d, at : at + ROWS, :] = q.astype(jnp.int16)
            codes += [code[:8], code[8:]]
        low = jnp.where(lane < 32, codes[0], codes[1])
        high = jnp.where(lane < 96, codes[2], codes[3])
        tile = jnp.where(lane < 64, low, high)
        out_ref[d, 4 * ROWS :, :] = tile.astype(jnp.int32).astype(jnp.int16)


def pack(residual, local_field, dests):
    block = pl.BlockSpec((ROWS, 32, LANES), lambda g: (0, g, 0))
    return pl.pallas_call(
        pack_body,
        grid=(dests // 16,),
        in_specs=[block, block],
        out_specs=pl.BlockSpec((16, 72, LANES), lambda g: (g, 0, 0)),
        out_shape=jax.ShapeDtypeStruct((dests, 72, LANES), jnp.int16),
        compiler_params=pltpu.CompilerParams(vmem_limit_bytes=32 << 20),
        name="pack",
    )(residual, local_field)


def conditional(options, step):
    for condition, source, to, sem in options:

        @pl.when(condition)
        def _():
            getattr(pltpu.make_async_copy(source, to, sem), step)()


def start_and_wait(options):
    conditional(options, "start")
    conditional(options, "wait")


def place_of(keeper, band):
    return jnp.where(keeper == band, 0, jnp.where(keeper == (band ^ 1), 1, 2))


def turn_body(slot, band_ref, keepers_ref, own_ref, twin_ref, out_ref, panel_ref, sem):
    tall = panel_ref.shape[0]
    band = band_ref[0]
    panel = (band & 1) ^ slot
    rows = pl.ds(pl.multiple_of(panel * tall, tall), tall)
    mine = place_of(keepers_ref[panel], band) == 0
    start_and_wait(
        [
            (mine, own_ref.at[rows], panel_ref, sem),
            (jnp.logical_not(mine), twin_ref.at[rows], panel_ref, sem),
        ]
    )
    out_ref[...] = panel_ref[...].T


def turn(slot, band, keepers, own, twin):
    anywhere = pl.BlockSpec(memory_space=pl.ANY)
    scalar = pl.BlockSpec(memory_space=pltpu.SMEM)
    rows, span = own.shape
    return pl.pallas_call(
        functools.partial(turn_body, slot),
        in_specs=[scalar, scalar, anywhere, anywhere],
        out_specs=pl.BlockSpec((span, rows // 2), lambda: (0, 0)),
        out_shape=jax.ShapeDtypeStruct((span, rows // 2), own.dtype),
        scratch_shapes=[pltpu.VMEM((rows // 2, span), own.dtype), pltpu.SemaphoreType.DMA],
        compiler_params=pltpu.CompilerParams(vmem_limit_bytes=16 << 20),
        name="turn",
    )(band, keepers, own, twin)


def kinetic_of(position):
    total = jnp.zeros(position.shape, jnp.int32)
    for index in (position >> 12, (position >> 6) & (GRID - 1), position & (GRID - 1)):
        folded = jnp.where(index >= GRID // 2, index - GRID, index)
        total = total + folded * folded
    return total.astype(jnp.float32) * (1.0 / (GRID * GRID))


def unpack(got_ref, hi_ref, lo_ref):
    sources = got_ref.shape[0]
    codes = got_ref[:, 4 * ROWS :, :].astype(jnp.int32).astype(jnp.float32)
    scales = jnp.exp2(codes * (1.0 / STEPS)) * (1.0 / TOP)
    for a in range(2):
        for p in range(2):
            at = p * 2 * ROWS + a * ROWS
            q = got_ref[:, at : at + ROWS, :].astype(jnp.int32).astype(jnp.float32)
            for r in range(2):
                col = 64 * a + 32 * r
                x = q[:, 8 * r : 8 * r + 8, :] * scales[:, :, col : col + 1]
                x = x.reshape(sources * 8, LANES)
                hi = x.astype(jnp.bfloat16)
                lo = (x - hi.astype(jnp.float32)).astype(jnp.bfloat16)
                hi_ref[a, r, :, p * LANES : (p + 1) * LANES] = hi
                lo_ref[a, r, :, p * LANES : (p + 1) * LANES] = lo


def rotate_body(
    band_ref, keepers_ref, lat_ref, got_ref, chip_ref, rest_ref, near_ref, far_ref, psi_ref, h_ref,
    psi_out, h_out, hi_ref, lo_ref, v_ref, state, v_sems, ins, outs
):
    planes, span, _ = psi_ref.shape
    tiles = outs.shape[1]
    tall = span // tiles
    depth = v_ref.shape[1] // 2

    band = band_ref[0]
    panels = []
    for p in range(2):
        here = place_of(keepers_ref[p], band) < 2
        to = v_ref.at[:, p * depth : (p + 1) * depth]
        for slot, refs in enumerate(((chip_ref, near_ref), (rest_ref, far_ref))):
            mine = (band & 1) ^ slot == p
            panels.append((mine & here, refs[0], to, v_sems.at[p]))
            panels.append((mine & jnp.logical_not(here), refs[1], to, v_sems.at[p]))

    def copies(refs, sems, inward):
        made = []
        for t in range(tiles):
            for s, ref in enumerate(refs):
                rows = pl.ds(t * tall, tall)
                ends = (ref.at[:, rows], state.at[s, :, rows])
                ends = ends if inward else ends[::-1]
                made.append(pltpu.make_async_copy(*ends, sems.at[s, t]))
        return made

    fetch = copies((psi_ref, h_ref), ins, True)
    store = copies((psi_out, h_out), outs, False)
    conditional(panels, "start")
    for copy in fetch:
        copy.start()
    kinetic = kinetic_of(lat_ref[...])
    unpack(got_ref, hi_ref, lo_ref)
    conditional(panels, "wait")
    for copy in fetch:
        copy.wait()
    for t in range(tiles):
        rows = slice(t * tall, (t + 1) * tall)
        v = v_ref[rows, :]

        def product(a, r):
            return jnp.dot(v, hi_ref[a, r], preferred_element_type=jnp.float32) + jnp.dot(
                v, lo_ref[a, r], preferred_element_type=jnp.float32
            )

        for r in range(planes):
            rotated = product(0, r)
            psi = state[0, r, rows].astype(jnp.float32)
            state[0, r, rows] = (psi + rotated).astype(jnp.bfloat16)
            applied = kinetic * rotated + product(1, r)
            h = state[1, r, rows].astype(jnp.float32)
            state[1, r, rows] = (h + applied).astype(jnp.bfloat16)
        store[2 * t].start()
        store[2 * t + 1].start()
    for copy in store:
        copy.wait()


def rotate(band, keepers, lattice, got, panels, psi, h):
    planes, span, width = psi.shape
    tiles = 8
    split = pltpu.VMEM((2, planes, got.shape[0] * 8, width), jnp.bfloat16)
    near = pl.BlockSpec(memory_space=pltpu.VMEM)
    far = pl.BlockSpec(memory_space=pl.ANY)
    scalar = pl.BlockSpec(memory_space=pltpu.SMEM)
    return pl.pallas_call(
        rotate_body,
        in_specs=[scalar, scalar, near, near] + [far] * 6,
        out_specs=[far, far],
        out_shape=[jax.ShapeDtypeStruct(psi.shape, psi.dtype)] * 2,
        scratch_shapes=[
            split,
            split,
            pltpu.VMEM((span, 2 * panels[0].shape[1]), panels[0].dtype),
            pltpu.VMEM((2,) + psi.shape, psi.dtype),
            pltpu.SemaphoreType.DMA((2,)),
            pltpu.SemaphoreType.DMA((2, tiles)),
            pltpu.SemaphoreType.DMA((2, tiles)),
        ],
        compiler_params=pltpu.CompilerParams(vmem_limit_bytes=52 << 20),
        name="rotate",
    )(band, keepers, lattice, got, *panels, psi, h)


def solution(mesh):
    n_pw = mesh.shape["pw"]
    n_band = mesh.shape["band"]

    def per_device(residual, local_field, orbital, energy, store, keepers, lattice):
        planes, vectors, _, waves = residual.shape
        width = waves // n_pw
        span = store.shape[2]
        band = lax.axis_index("band").reshape(1)

        swap = [(b, b ^ 1) for b in range(n_band)]
        across = [
            (p * n_band + b, (p ^ (n_pw // 2)) * n_band + (b ^ 2))
            for p in range(n_pw)
            for b in range(n_band)
        ]
        own = store[0]
        twin = lax.ppermute(own, "band", swap)
        chip = turn(0, band, keepers, own, twin)
        near = lax.ppermute(chip, ("pw", "band"), across)
        rest = turn(1, band, keepers, own, twin)
        far = lax.ppermute(near, "band", swap)

        rows = planes * vectors
        flat = (rows, waves // LANES, LANES)
        sent = pack(residual.reshape(flat), local_field.reshape(flat), n_pw)
        got = lax.all_to_all(sent, "pw", split_axis=0, concat_axis=0, tiled=True)

        shape = (planes, span, width)
        psi, h = rotate(
            band, keepers, lattice, got, (chip, rest, near, far), orbital.reshape(shape), energy.reshape(shape)
        )
        return psi.reshape(orbital.shape), h.reshape(energy.shape)

    in_specs = (
        P(None, "pw", "band", None),
        P(None, "pw", "band", None),
        P(None, None, "band", "pw"),
        P(None, None, "band", "pw"),
        P("band", None, None),
        P(),
        P("band", "pw"),
    )
    out_specs = (P(None, None, "band", "pw"), P(None, None, "band", "pw"))
    return jax.shard_map(
        per_device, mesh=mesh, in_specs=in_specs, out_specs=out_specs, check_vma=False
    )
```

```python
import functools

import jax
import jax.numpy as jnp
from jax import lax
from jax.experimental import pallas as pl
from jax.experimental.pallas import tpu as pltpu
from jax.sharding import PartitionSpec as P

GRID = 64
LANES = 128
ROWS = 16
STEPS = 256.0
TOP = 32600.0
TILES = (640, 640, 512, 256)


def pack_body(r_ref, l_ref, out_ref, fields, sent, ins, outs):
    chunks = outs.shape[0]
    dests = sent.shape[0] // chunks
    stride = 2 * dests

    fetch = [
        [
            pltpu.make_async_copy(ref.at[:, pl.ds(c * stride, stride)], fields.at[c, a], ins.at[c, a])
            for a, ref in enumerate((r_ref, l_ref))
        ]
        for c in range(chunks)
    ]
    store = []
    for c in range(chunks):
        for copy in fetch[c]:
            copy.start()
        some = pl.ds(c * dests, dests)
        store.append(pltpu.make_async_copy(sent.at[some], out_ref.at[some], outs.at[c]))

    lane = lax.broadcasted_iota(jnp.int32, (8, LANES), 1)
    for c in range(chunks):
        for copy in fetch[c]:
            copy.wait()
        for d in range(dests):
            codes = []
            for a in range(2):
                ref = fields.at[c, a].reshape(ROWS * stride, LANES)
                halves = [ref[pl.ds(2 * d + p, ROWS, stride=stride), :] for p in range(2)]
                top = jnp.maximum(jnp.abs(halves[0]), jnp.abs(halves[1]))
                top = jnp.max(top, axis=1, keepdims=True)
                code = jnp.ceil(jnp.log2(jnp.maximum(top, 1e-30)) * STEPS) + 1.0
                inverse = jnp.exp2(code * (-1.0 / STEPS)) * TOP
                for p in range(2):
                    q = jnp.round(halves[p] * inverse).astype(jnp.int32)
                    at = p * 2 * ROWS + a * ROWS
                    sent[c * dests + d, at : at + ROWS, :] = q.astype(jnp.int16)
                codes += [code[:8], code[8:]]
            low = jnp.where(lane < 32, codes[0], codes[1])
            high = jnp.where(lane < 96, codes[2], codes[3])
            tile = jnp.where(lane < 64, low, high)
            sent[c * dests + d, 4 * ROWS :, :] = tile.astype(jnp.int32).astype(jnp.int16)
        store[c].start()
    for copy in store:
        copy.wait()


def pack(residual, local_field, dests):
    chunks = 8
    anywhere = pl.BlockSpec(memory_space=pl.ANY)
    rows = residual.shape[1] // chunks
    return pl.pallas_call(
        pack_body,
        in_specs=[anywhere, anywhere],
        out_specs=anywhere,
        out_shape=jax.ShapeDtypeStruct((dests, 72, LANES), jnp.int16),
        scratch_shapes=[
            pltpu.VMEM((chunks, 2, ROWS, rows, LANES), jnp.float32),
            pltpu.VMEM((dests, 72, LANES), jnp.int16),
            pltpu.SemaphoreType.DMA((chunks, 2)),
            pltpu.SemaphoreType.DMA((chunks,)),
        ],
        compiler_params=pltpu.CompilerParams(vmem_limit_bytes=58 << 20),
        name="pack",
    )(residual, local_field)


def conditional(options, step):
    for condition, source, to, sem in options:

        @pl.when(condition)
        def _():
            getattr(pltpu.make_async_copy(source, to, sem), step)()


def start_and_wait(options):
    conditional(options, "start")
    conditional(options, "wait")


def place_of(keeper, band):
    return jnp.where(keeper == band, 0, jnp.where(keeper == (band ^ 1), 1, 2))


def turn_body(slot, band_ref, keepers_ref, own_ref, twin_ref, out_ref, panel_ref, sem):
    tall = panel_ref.shape[0]
    band = band_ref[0]
    panel = (band & 1) ^ slot
    rows = pl.ds(pl.multiple_of(panel * tall, tall), tall)
    mine = place_of(keepers_ref[panel], band) == 0
    start_and_wait(
        [
            (mine, own_ref.at[rows], panel_ref, sem),
            (jnp.logical_not(mine), twin_ref.at[rows], panel_ref, sem),
        ]
    )
    out_ref[...] = panel_ref[...].T


def turn(slot, band, keepers, own, twin):
    anywhere = pl.BlockSpec(memory_space=pl.ANY)
    scalar = pl.BlockSpec(memory_space=pltpu.SMEM)
    rows, span = own.shape
    return pl.pallas_call(
        functools.partial(turn_body, slot),
        in_specs=[scalar, scalar, anywhere, anywhere],
        out_specs=pl.BlockSpec((span, rows // 2), lambda: (0, 0)),
        out_shape=jax.ShapeDtypeStruct((span, rows // 2), own.dtype),
        scratch_shapes=[pltpu.VMEM((rows // 2, span), own.dtype), pltpu.SemaphoreType.DMA],
        compiler_params=pltpu.CompilerParams(vmem_limit_bytes=16 << 20),
        name="turn",
    )(band, keepers, own, twin)


def kinetic_of(position):
    total = jnp.zeros(position.shape, jnp.int32)
    for index in (position >> 12, (position >> 6) & (GRID - 1), position & (GRID - 1)):
        folded = jnp.where(index >= GRID // 2, index - GRID, index)
        total = total + folded * folded
    return total.astype(jnp.float32) * (1.0 / (GRID * GRID))


def unpack(got_ref, hi_ref, lo_ref):
    sources = got_ref.shape[0]
    codes = got_ref[:, 4 * ROWS :, :].astype(jnp.int32).astype(jnp.float32)
    scales = jnp.exp2(codes * (1.0 / STEPS)) * (1.0 / TOP)
    for a in range(2):
        for p in range(2):
            at = p * 2 * ROWS + a * ROWS
            q = got_ref[:, at : at + ROWS, :].astype(jnp.int32).astype(jnp.float32)
            for r in range(2):
                col = 64 * a + 32 * r
                x = q[:, 8 * r : 8 * r + 8, :] * scales[:, :, col : col + 1]
                x = x.reshape(sources * 8, LANES)
                hi = x.astype(jnp.bfloat16)
                lo = (x - hi.astype(jnp.float32)).astype(jnp.bfloat16)
                hi_ref[a, r, :, p * LANES : (p + 1) * LANES] = hi
                lo_ref[a, r, :, p * LANES : (p + 1) * LANES] = lo


def rotate_body(
    band_ref, keepers_ref, lat_ref, got_hbm, chip_ref, rest_ref, near_ref, far_ref, psi_ref, h_ref,
    psi_out, h_out, got_ref, hi_ref, lo_ref, v_ref, state, got_sem, v_sems, ins, outs
):
    tiles = len(TILES)
    starts = [sum(TILES[:t]) for t in range(tiles)]
    planes = psi_ref.shape[0]
    depth = v_ref.shape[1] // 2

    band = band_ref[0]
    panels = []
    for t in range(tiles):
        rows = pl.ds(starts[t], TILES[t])
        options = []
        for p in range(2):
            here = place_of(keepers_ref[p], band) < 2
            to = v_ref.at[rows, p * depth : (p + 1) * depth]
            for slot, refs in enumerate(((chip_ref, near_ref), (rest_ref, far_ref))):
                mine = (band & 1) ^ slot == p
                options.append((mine & here, refs[0].at[rows], to, v_sems.at[t, p]))
                options.append((mine & jnp.logical_not(here), refs[1].at[rows], to, v_sems.at[t, p]))
        panels.append(options)

    def copies(refs, sems, inward):
        made = []
        for t in range(tiles):
            for s, ref in enumerate(refs):
                rows = pl.ds(starts[t], TILES[t])
                ends = (ref.at[:, rows], state.at[s, :, rows])
                ends = ends if inward else ends[::-1]
                made.append(pltpu.make_async_copy(*ends, sems.at[s, t]))
        return made

    fetch = copies((psi_ref, h_ref), ins, True)
    store = copies((psi_out, h_out), outs, False)
    message = pltpu.make_async_copy(got_hbm, got_ref, got_sem)
    message.start()
    for t in range(tiles):
        conditional(panels[t], "start")
        for s in range(2):
            fetch[2 * t + s].start()
    kinetic = kinetic_of(lat_ref[...])
    message.wait()
    unpack(got_ref, hi_ref, lo_ref)
    for t in range(tiles):
        conditional(panels[t], "wait")
        for s in range(2):
            fetch[2 * t + s].wait()
        rows = slice(starts[t], starts[t] + TILES[t])
        v = v_ref[rows, :]

        def product(a, r):
            return jnp.dot(v, hi_ref[a, r], preferred_element_type=jnp.float32) + jnp.dot(
                v, lo_ref[a, r], preferred_element_type=jnp.float32
            )

        for r in range(planes):
            rotated = product(0, r)
            psi = state[0, r, rows].astype(jnp.float32)
            state[0, r, rows] = (psi + rotated).astype(jnp.bfloat16)
            applied = kinetic * rotated + product(1, r)
            h = state[1, r, rows].astype(jnp.float32)
            state[1, r, rows] = (h + applied).astype(jnp.bfloat16)
        store[2 * t].start()
        store[2 * t + 1].start()
    for copy in store:
        copy.wait()


def rotate(band, keepers, lattice, got, panels, psi, h):
    planes, span, width = psi.shape
    assert sum(TILES) == span
    tiles = len(TILES)
    split = pltpu.VMEM((2, planes, got.shape[0] * 8, width), jnp.bfloat16)
    near = pl.BlockSpec(memory_space=pltpu.VMEM)
    far = pl.BlockSpec(memory_space=pl.ANY)
    scalar = pl.BlockSpec(memory_space=pltpu.SMEM)
    return pl.pallas_call(
        rotate_body,
        in_specs=[scalar, scalar, near] + [far] * 7,
        out_specs=[far, far],
        out_shape=[jax.ShapeDtypeStruct(psi.shape, psi.dtype)] * 2,
        scratch_shapes=[
            pltpu.VMEM(got.shape, got.dtype),
            split,
            split,
            pltpu.VMEM((span, 2 * panels[0].shape[1]), panels[0].dtype),
            pltpu.VMEM((2,) + psi.shape, psi.dtype),
            pltpu.SemaphoreType.DMA,
            pltpu.SemaphoreType.DMA((tiles, 2)),
            pltpu.SemaphoreType.DMA((2, tiles)),
            pltpu.SemaphoreType.DMA((2, tiles)),
        ],
        compiler_params=pltpu.CompilerParams(vmem_limit_bytes=52 << 20),
        name="rotate",
    )(band, keepers, lattice, got, *panels, psi, h)


def solution(mesh):
    n_pw = mesh.shape["pw"]
    n_band = mesh.shape["band"]

    def per_device(residual, local_field, orbital, energy, store, keepers, lattice):
        planes, vectors, _, waves = residual.shape
        width = waves // n_pw
        span = store.shape[2]
        band = lax.axis_index("band").reshape(1)

        swap = [(b, b ^ 1) for b in range(n_band)]
        across = [
            (p * n_band + b, (p ^ (n_pw // 2)) * n_band + (b ^ 2))
            for p in range(n_pw)
            for b in range(n_band)
        ]
        own = store[0]
        twin = lax.ppermute(own, "band", swap)
        chip = turn(0, band, keepers, own, twin)
        near = lax.ppermute(chip, ("pw", "band"), across)
        rest = turn(1, band, keepers, own, twin)
        far = lax.ppermute(near, "band", swap)

        rows = planes * vectors
        flat = (rows, waves // LANES, LANES)
        sent = pack(residual.reshape(flat), local_field.reshape(flat), n_pw)
        got = lax.all_to_all(sent, "pw", split_axis=0, concat_axis=0, tiled=True)

        shape = (planes, span, width)
        psi, h = rotate(
            band, keepers, lattice, got, (chip, rest, near, far), orbital.reshape(shape), energy.reshape(shape)
        )
        return psi.reshape(orbital.shape), h.reshape(energy.shape)

    in_specs = (
        P(None, "pw", "band", None),
        P(None, "pw", "band", None),
        P(None, None, "band", "pw"),
        P(None, None, "band", "pw"),
        P("band", None, None),
        P(),
        P("band", "pw"),
    )
    out_specs = (P(None, None, "band", "pw"), P(None, None, "band", "pw"))
    return jax.shard_map(
        per_device, mesh=mesh, in_specs=in_specs, out_specs=out_specs, check_vma=False
    )
```

```python
import functools

import jax
import jax.numpy as jnp
from jax import lax
from jax.experimental import pallas as pl
from jax.experimental.pallas import tpu as pltpu
from jax.sharding import PartitionSpec as P

GRID = 64
LANES = 128
ROWS = 16
STEPS = 256.0
TOP = 32600.0
TILES = (640, 640, 512, 256)


def pack_body(r_ref, l_ref, out_ref, fields, sent, ins, outs):
    chunks = outs.shape[0]
    dests = sent.shape[0] // chunks
    stride = 2 * dests

    fetch = [
        [
            pltpu.make_async_copy(ref.at[:, pl.ds(c * stride, stride)], fields.at[c, a], ins.at[c, a])
            for a, ref in enumerate((r_ref, l_ref))
        ]
        for c in range(chunks)
    ]
    store = []
    for c in range(chunks):
        for copy in fetch[c]:
            copy.start()
        some = pl.ds(c * dests, dests)
        store.append(pltpu.make_async_copy(sent.at[some], out_ref.at[some], outs.at[c]))

    lane = lax.broadcasted_iota(jnp.int32, (8, LANES), 1)
    for c in range(chunks):
        for copy in fetch[c]:
            copy.wait()
        for d in range(dests):
            codes = []
            for a in range(2):
                ref = fields.at[c, a].reshape(ROWS * stride, LANES)
                halves = [ref[pl.ds(2 * d + p, ROWS, stride=stride), :] for p in range(2)]
                top = jnp.maximum(jnp.abs(halves[0]), jnp.abs(halves[1]))
                top = jnp.max(top, axis=1, keepdims=True)
                code = jnp.ceil(jnp.log2(jnp.maximum(top, 1e-30)) * STEPS) + 1.0
                inverse = jnp.exp2(code * (-1.0 / STEPS)) * TOP
                for p in range(2):
                    q = jnp.round(halves[p] * inverse).astype(jnp.int32)
                    at = p * 2 * ROWS + a * ROWS
                    sent[c * dests + d, at : at + ROWS, :] = q.astype(jnp.int16)
                codes += [code[:8], code[8:]]
            low = jnp.where(lane < 32, codes[0], codes[1])
            high = jnp.where(lane < 96, codes[2], codes[3])
            tile = jnp.where(lane < 64, low, high)
            sent[c * dests + d, 4 * ROWS :, :] = tile.astype(jnp.int32).astype(jnp.int16)
        store[c].start()
    for copy in store:
        copy.wait()


def pack(residual, local_field, dests):
    chunks = 8
    anywhere = pl.BlockSpec(memory_space=pl.ANY)
    rows = residual.shape[1] // chunks
    return pl.pallas_call(
        pack_body,
        in_specs=[anywhere, anywhere],
        out_specs=anywhere,
        out_shape=jax.ShapeDtypeStruct((dests, 72, LANES), jnp.int16),
        scratch_shapes=[
            pltpu.VMEM((chunks, 2, ROWS, rows, LANES), jnp.float32),
            pltpu.VMEM((dests, 72, LANES), jnp.int16),
            pltpu.SemaphoreType.DMA((chunks, 2)),
            pltpu.SemaphoreType.DMA((chunks,)),
        ],
        compiler_params=pltpu.CompilerParams(vmem_limit_bytes=58 << 20),
        name="pack",
    )(residual, local_field)


def conditional(options, step):
    for condition, source, to, sem in options:

        @pl.when(condition)
        def _():
            getattr(pltpu.make_async_copy(source, to, sem), step)()


def start_and_wait(options):
    conditional(options, "start")
    conditional(options, "wait")


def place_of(keeper, band):
    return jnp.where(keeper == band, 0, jnp.where(keeper == (band ^ 1), 1, 2))


def turn_body(slot, band_ref, keepers_ref, own_ref, twin_ref, out_ref, panel_ref, sem):
    tall = panel_ref.shape[0]
    band = band_ref[0]
    panel = (band & 1) ^ slot
    rows = pl.ds(pl.multiple_of(panel * tall, tall), tall)
    mine = place_of(keepers_ref[panel], band) == 0
    start_and_wait(
        [
            (mine, own_ref.at[rows], panel_ref, sem),
            (jnp.logical_not(mine), twin_ref.at[rows], panel_ref, sem),
        ]
    )
    out_ref[...] = panel_ref[...].T


def turn(slot, band, keepers, own, twin):
    anywhere = pl.BlockSpec(memory_space=pl.ANY)
    scalar = pl.BlockSpec(memory_space=pltpu.SMEM)
    rows, span = own.shape
    return pl.pallas_call(
        functools.partial(turn_body, slot),
        in_specs=[scalar, scalar, anywhere, anywhere],
        out_specs=pl.BlockSpec((span, rows // 2), lambda: (0, 0)),
        out_shape=jax.ShapeDtypeStruct((span, rows // 2), own.dtype),
        scratch_shapes=[pltpu.VMEM((rows // 2, span), own.dtype), pltpu.SemaphoreType.DMA],
        compiler_params=pltpu.CompilerParams(vmem_limit_bytes=(16 if slot == 0 else 58) << 20),
        name="turn",
    )(band, keepers, own, twin)


def kinetic_of(position):
    total = jnp.zeros(position.shape, jnp.int32)
    for index in (position >> 12, (position >> 6) & (GRID - 1), position & (GRID - 1)):
        folded = jnp.where(index >= GRID // 2, index - GRID, index)
        total = total + folded * folded
    return total.astype(jnp.float32) * (1.0 / (GRID * GRID))


def unpack(got_ref, hi_ref, lo_ref):
    sources = got_ref.shape[0]
    codes = got_ref[:, 4 * ROWS :, :].astype(jnp.int32).astype(jnp.float32)
    scales = jnp.exp2(codes * (1.0 / STEPS)) * (1.0 / TOP)
    for a in range(2):
        for p in range(2):
            at = p * 2 * ROWS + a * ROWS
            q = got_ref[:, at : at + ROWS, :].astype(jnp.int32).astype(jnp.float32)
            for r in range(2):
                col = 64 * a + 32 * r
                x = q[:, 8 * r : 8 * r + 8, :] * scales[:, :, col : col + 1]
                x = x.reshape(sources * 8, LANES)
                hi = x.astype(jnp.bfloat16)
                lo = (x - hi.astype(jnp.float32)).astype(jnp.bfloat16)
                hi_ref[a, r, :, p * LANES : (p + 1) * LANES] = hi
                lo_ref[a, r, :, p * LANES : (p + 1) * LANES] = lo


def rotate_body(
    band_ref, keepers_ref, lat_ref, got_hbm, chip_ref, rest_ref, near_ref, far_ref, psi_ref, h_ref,
    psi_out, h_out, got_ref, hi_ref, lo_ref, v_ref, state, got_sem, v_sems, ins, outs
):
    tiles = len(TILES)
    starts = [sum(TILES[:t]) for t in range(tiles)]
    planes = psi_ref.shape[0]
    depth = v_ref.shape[1] // 2

    band = band_ref[0]
    panels = []
    for t in range(tiles):
        rows = pl.ds(starts[t], TILES[t])
        options = []
        for p in range(2):
            here = place_of(keepers_ref[p], band) < 2
            to = v_ref.at[rows, p * depth : (p + 1) * depth]
            for slot, refs in enumerate(((chip_ref, near_ref), (rest_ref, far_ref))):
                mine = (band & 1) ^ slot == p
                options.append((mine & here, refs[0].at[rows], to, v_sems.at[t, p]))
                options.append((mine & jnp.logical_not(here), refs[1].at[rows], to, v_sems.at[t, p]))
        panels.append(options)

    def copies(refs, sems, inward):
        made = []
        for t in range(tiles):
            for s, ref in enumerate(refs):
                rows = pl.ds(starts[t], TILES[t])
                ends = (ref.at[:, rows], state.at[s, :, rows])
                ends = ends if inward else ends[::-1]
                made.append(pltpu.make_async_copy(*ends, sems.at[s, t]))
        return made

    fetch = copies((psi_ref, h_ref), ins, True)
    store = copies((psi_out, h_out), outs, False)
    message = pltpu.make_async_copy(got_hbm, got_ref, got_sem)
    message.start()
    for t in range(tiles):
        conditional(panels[t], "start")
        for s in range(2):
            fetch[2 * t + s].start()
    kinetic = kinetic_of(lat_ref[...])
    message.wait()
    unpack(got_ref, hi_ref, lo_ref)
    for t in range(tiles):
        conditional(panels[t], "wait")
        for s in range(2):
            fetch[2 * t + s].wait()
        rows = slice(starts[t], starts[t] + TILES[t])
        v = v_ref[rows, :]

        def product(a, r):
            return jnp.dot(v, hi_ref[a, r], preferred_element_type=jnp.float32) + jnp.dot(
                v, lo_ref[a, r], preferred_element_type=jnp.float32
            )

        for r in range(planes):
            rotated = product(0, r)
            psi = state[0, r, rows].astype(jnp.float32)
            state[0, r, rows] = (psi + rotated).astype(jnp.bfloat16)
            applied = kinetic * rotated + product(1, r)
            h = state[1, r, rows].astype(jnp.float32)
            state[1, r, rows] = (h + applied).astype(jnp.bfloat16)
        store[2 * t].start()
        store[2 * t + 1].start()
    for copy in store:
        copy.wait()


def rotate(band, keepers, lattice, got, panels, psi, h):
    planes, span, width = psi.shape
    assert sum(TILES) == span
    tiles = len(TILES)
    split = pltpu.VMEM((2, planes, got.shape[0] * 8, width), jnp.bfloat16)
    near = pl.BlockSpec(memory_space=pltpu.VMEM)
    far = pl.BlockSpec(memory_space=pl.ANY)
    scalar = pl.BlockSpec(memory_space=pltpu.SMEM)
    return pl.pallas_call(
        rotate_body,
        in_specs=[scalar, scalar, near] + [far] * 7,
        out_specs=[far, far],
        out_shape=[jax.ShapeDtypeStruct(psi.shape, psi.dtype)] * 2,
        scratch_shapes=[
            pltpu.VMEM(got.shape, got.dtype),
            split,
            split,
            pltpu.VMEM((span, 2 * panels[0].shape[1]), panels[0].dtype),
            pltpu.VMEM((2,) + psi.shape, psi.dtype),
            pltpu.SemaphoreType.DMA,
            pltpu.SemaphoreType.DMA((tiles, 2)),
            pltpu.SemaphoreType.DMA((2, tiles)),
            pltpu.SemaphoreType.DMA((2, tiles)),
        ],
        compiler_params=pltpu.CompilerParams(vmem_limit_bytes=52 << 20),
        name="rotate",
    )(band, keepers, lattice, got, *panels, psi, h)


def solution(mesh):
    n_pw = mesh.shape["pw"]
    n_band = mesh.shape["band"]

    def per_device(residual, local_field, orbital, energy, store, keepers, lattice):
        planes, vectors, _, waves = residual.shape
        width = waves // n_pw
        span = store.shape[2]
        band = lax.axis_index("band").reshape(1)

        swap = [(b, b ^ 1) for b in range(n_band)]
        across = [
            (p * n_band + b, (p ^ (n_pw // 2)) * n_band + (b ^ 2))
            for p in range(n_pw)
            for b in range(n_band)
        ]
        own = store[0]
        twin = lax.ppermute(own, "band", swap)
        chip = turn(0, band, keepers, own, twin)
        near = lax.ppermute(chip, ("pw", "band"), across)
        rest = turn(1, band, keepers, own, twin)
        near, rest = lax.optimization_barrier((near, rest))
        far = lax.ppermute(near, "band", swap)

        rows = planes * vectors
        flat = (rows, waves // LANES, LANES)
        sent = pack(residual.reshape(flat), local_field.reshape(flat), n_pw)
        got = lax.all_to_all(sent, "pw", split_axis=0, concat_axis=0, tiled=True)

        shape = (planes, span, width)
        psi, h = rotate(
            band, keepers, lattice, got, (chip, rest, near, far), orbital.reshape(shape), energy.reshape(shape)
        )
        return psi.reshape(orbital.shape), h.reshape(energy.shape)

    in_specs = (
        P(None, "pw", "band", None),
        P(None, "pw", "band", None),
        P(None, None, "band", "pw"),
        P(None, None, "band", "pw"),
        P("band", None, None),
        P(),
        P("band", "pw"),
    )
    out_specs = (P(None, None, "band", "pw"), P(None, None, "band", "pw"))
    return jax.shard_map(
        per_device, mesh=mesh, in_specs=in_specs, out_specs=out_specs, check_vma=False
    )
```

```python
import functools

import jax
import jax.numpy as jnp
from jax import lax
from jax.experimental import pallas as pl
from jax.experimental.pallas import tpu as pltpu
from jax.sharding import PartitionSpec as P

GRID = 64
LANES = 128
ROWS = 16
STEPS = 256.0
TOP = 32600.0
TILES = (640, 640, 512, 256)


def pack_body(r_ref, l_ref, out_ref, fields, sent, ins, outs):
    chunks = outs.shape[0]
    dests = sent.shape[0] // chunks
    stride = 2 * dests

    fetch = [
        [
            pltpu.make_async_copy(ref.at[:, pl.ds(c * stride, stride)], fields.at[c, a], ins.at[c, a])
            for a, ref in enumerate((r_ref, l_ref))
        ]
        for c in range(chunks)
    ]
    store = []
    for c in range(chunks):
        for copy in fetch[c]:
            copy.start()
        some = pl.ds(c * dests, dests)
        store.append(pltpu.make_async_copy(sent.at[some], out_ref.at[some], outs.at[c]))

    lane = lax.broadcasted_iota(jnp.int32, (8, LANES), 1)
    for c in range(chunks):
        for copy in fetch[c]:
            copy.wait()
        for d in range(dests):
            codes = []
            for a in range(2):
                ref = fields.at[c, a].reshape(ROWS * stride, LANES)
                halves = [ref[pl.ds(2 * d + p, ROWS, stride=stride), :] for p in range(2)]
                top = jnp.maximum(jnp.abs(halves[0]), jnp.abs(halves[1]))
                top = jnp.max(top, axis=1, keepdims=True)
                code = jnp.ceil(jnp.log2(jnp.maximum(top, 1e-30)) * STEPS) + 1.0
                inverse = jnp.exp2(code * (-1.0 / STEPS)) * TOP
                for p in range(2):
                    q = jnp.round(halves[p] * inverse).astype(jnp.int32)
                    at = p * 2 * ROWS + a * ROWS
                    sent[c * dests + d, at : at + ROWS, :] = q.astype(jnp.int16)
                codes += [code[:8], code[8:]]
            low = jnp.where(lane < 32, codes[0], codes[1])
            high = jnp.where(lane < 96, codes[2], codes[3])
            tile = jnp.where(lane < 64, low, high)
            sent[c * dests + d, 4 * ROWS :, :] = tile.astype(jnp.int32).astype(jnp.int16)
        store[c].start()
    for copy in store:
        copy.wait()


def pack(residual, local_field, dests):
    chunks = 8
    anywhere = pl.BlockSpec(memory_space=pl.ANY)
    rows = residual.shape[1] // chunks
    return pl.pallas_call(
        pack_body,
        in_specs=[anywhere, anywhere],
        out_specs=anywhere,
        out_shape=jax.ShapeDtypeStruct((dests, 72, LANES), jnp.int16),
        scratch_shapes=[
            pltpu.VMEM((chunks, 2, ROWS, rows, LANES), jnp.float32),
            pltpu.VMEM((dests, 72, LANES), jnp.int16),
            pltpu.SemaphoreType.DMA((chunks, 2)),
            pltpu.SemaphoreType.DMA((chunks,)),
        ],
        compiler_params=pltpu.CompilerParams(vmem_limit_bytes=58 << 20),
        name="pack",
    )(residual, local_field)


def conditional(options, step):
    for condition, source, to, sem in options:

        @pl.when(condition)
        def _():
            getattr(pltpu.make_async_copy(source, to, sem), step)()


def start_and_wait(options):
    conditional(options, "start")
    conditional(options, "wait")


def place_of(keeper, band):
    return jnp.where(keeper == band, 0, jnp.where(keeper == (band ^ 1), 1, 2))


def turn_body(slot, band_ref, keepers_ref, own_ref, twin_ref, out_ref, panel_ref, sem):
    tall = panel_ref.shape[0]
    band = band_ref[0]
    panel = (band & 1) ^ slot
    rows = pl.ds(pl.multiple_of(panel * tall, tall), tall)
    mine = place_of(keepers_ref[panel], band) == 0
    start_and_wait(
        [
            (mine, own_ref.at[rows], panel_ref, sem),
            (jnp.logical_not(mine), twin_ref.at[rows], panel_ref, sem),
        ]
    )
    out_ref[...] = panel_ref[...].T


def turn(slot, band, keepers, own, twin):
    anywhere = pl.BlockSpec(memory_space=pl.ANY)
    scalar = pl.BlockSpec(memory_space=pltpu.SMEM)
    rows, span = own.shape
    return pl.pallas_call(
        functools.partial(turn_body, slot),
        in_specs=[scalar, scalar, anywhere, anywhere],
        out_specs=pl.BlockSpec((span, rows // 2), lambda: (0, 0)),
        out_shape=jax.ShapeDtypeStruct((span, rows // 2), own.dtype),
        scratch_shapes=[pltpu.VMEM((rows // 2, span), own.dtype), pltpu.SemaphoreType.DMA],
        compiler_params=pltpu.CompilerParams(vmem_limit_bytes=(16 if slot == 0 else 58) << 20),
        name="turn",
    )(band, keepers, own, twin)


def kinetic_of(position):
    total = jnp.zeros(position.shape, jnp.int32)
    for index in (position >> 12, (position >> 6) & (GRID - 1), position & (GRID - 1)):
        folded = jnp.where(index >= GRID // 2, index - GRID, index)
        total = total + folded * folded
    return total.astype(jnp.float32) * (1.0 / (GRID * GRID))


def unpack(got_ref, hi_ref, lo_ref):
    sources = got_ref.shape[0]
    codes = got_ref[:, 4 * ROWS :, :].astype(jnp.int32).astype(jnp.float32)
    scales = jnp.exp2(codes * (1.0 / STEPS)) * (1.0 / TOP)
    for a in range(2):
        for p in range(2):
            at = p * 2 * ROWS + a * ROWS
            q = got_ref[:, at : at + ROWS, :].astype(jnp.int32).astype(jnp.float32)
            for r in range(2):
                col = 64 * a + 32 * r
                x = q[:, 8 * r : 8 * r + 8, :] * scales[:, :, col : col + 1]
                x = x.reshape(sources * 8, LANES)
                hi = x.astype(jnp.bfloat16)
                lo = (x - hi.astype(jnp.float32)).astype(jnp.bfloat16)
                hi_ref[a, r, :, p * LANES : (p + 1) * LANES] = hi
                lo_ref[a, r, :, p * LANES : (p + 1) * LANES] = lo


def rotate_body(
    band_ref, keepers_ref, lat_ref, got_hbm, chip_ref, rest_ref, near_ref, far_ref, psi_ref, h_ref,
    psi_out, h_out, got_ref, hi_ref, lo_ref, v_ref, state, got_sem, v_sems, ins, outs
):
    tiles = len(TILES)
    starts = [sum(TILES[:t]) for t in range(tiles)]
    planes = psi_ref.shape[0]
    depth = v_ref.shape[1] // 2

    band = band_ref[0]
    panels = []
    for t in range(tiles):
        rows = pl.ds(starts[t], TILES[t])
        options = []
        for p in range(2):
            here = place_of(keepers_ref[p], band) < 2
            to = v_ref.at[rows, p * depth : (p + 1) * depth]
            for slot, refs in enumerate(((chip_ref, near_ref), (rest_ref, far_ref))):
                mine = (band & 1) ^ slot == p
                options.append((mine & here, refs[0].at[rows], to, v_sems.at[t, p]))
                options.append((mine & jnp.logical_not(here), refs[1].at[rows], to, v_sems.at[t, p]))
        panels.append(options)

    def copies(refs, sems, inward):
        made = []
        for t in range(tiles):
            for s, ref in enumerate(refs):
                rows = pl.ds(starts[t], TILES[t])
                ends = (ref.at[:, rows], state.at[s, :, rows])
                ends = ends if inward else ends[::-1]
                made.append(pltpu.make_async_copy(*ends, sems.at[s, t]))
        return made

    fetch = copies((psi_ref, h_ref), ins, True)
    store = copies((psi_out, h_out), outs, False)
    message = pltpu.make_async_copy(got_hbm, got_ref, got_sem)
    message.start()
    for t in range(tiles):
        conditional(panels[t], "start")
        for s in range(2):
            fetch[2 * t + s].start()
    kinetic = kinetic_of(lat_ref[...])
    message.wait()
    unpack(got_ref, hi_ref, lo_ref)
    for t in range(tiles):
        conditional(panels[t], "wait")
        for s in range(2):
            fetch[2 * t + s].wait()
        rows = slice(starts[t], starts[t] + TILES[t])
        twice = jnp.concatenate([v_ref[rows, :]] * 2, axis=1)

        def product(a, r):
            parts = jnp.concatenate([hi_ref[a, r], lo_ref[a, r]], axis=0)
            return jnp.dot(twice, parts, preferred_element_type=jnp.float32)

        for r in range(planes):
            rotated = product(0, r)
            psi = state[0, r, rows].astype(jnp.float32)
            state[0, r, rows] = (psi + rotated).astype(jnp.bfloat16)
            applied = kinetic * rotated + product(1, r)
            h = state[1, r, rows].astype(jnp.float32)
            state[1, r, rows] = (h + applied).astype(jnp.bfloat16)
        store[2 * t].start()
        store[2 * t + 1].start()
    for copy in store:
        copy.wait()


def rotate(band, keepers, lattice, got, panels, psi, h):
    planes, span, width = psi.shape
    assert sum(TILES) == span
    tiles = len(TILES)
    split = pltpu.VMEM((2, planes, got.shape[0] * 8, width), jnp.bfloat16)
    near = pl.BlockSpec(memory_space=pltpu.VMEM)
    far = pl.BlockSpec(memory_space=pl.ANY)
    scalar = pl.BlockSpec(memory_space=pltpu.SMEM)
    return pl.pallas_call(
        rotate_body,
        in_specs=[scalar, scalar, near] + [far] * 7,
        out_specs=[far, far],
        out_shape=[jax.ShapeDtypeStruct(psi.shape, psi.dtype)] * 2,
        scratch_shapes=[
            pltpu.VMEM(got.shape, got.dtype),
            split,
            split,
            pltpu.VMEM((span, 2 * panels[0].shape[1]), panels[0].dtype),
            pltpu.VMEM((2,) + psi.shape, psi.dtype),
            pltpu.SemaphoreType.DMA,
            pltpu.SemaphoreType.DMA((tiles, 2)),
            pltpu.SemaphoreType.DMA((2, tiles)),
            pltpu.SemaphoreType.DMA((2, tiles)),
        ],
        compiler_params=pltpu.CompilerParams(vmem_limit_bytes=52 << 20),
        name="rotate",
    )(band, keepers, lattice, got, *panels, psi, h)


def solution(mesh):
    n_pw = mesh.shape["pw"]
    n_band = mesh.shape["band"]

    def per_device(residual, local_field, orbital, energy, store, keepers, lattice):
        planes, vectors, _, waves = residual.shape
        width = waves // n_pw
        span = store.shape[2]
        band = lax.axis_index("band").reshape(1)

        swap = [(b, b ^ 1) for b in range(n_band)]
        across = [
            (p * n_band + b, (p ^ (n_pw // 2)) * n_band + (b ^ 2))
            for p in range(n_pw)
            for b in range(n_band)
        ]
        own = store[0]
        twin = lax.ppermute(own, "band", swap)
        chip = turn(0, band, keepers, own, twin)
        near = lax.ppermute(chip, ("pw", "band"), across)
        rest = turn(1, band, keepers, own, twin)
        near, rest = lax.optimization_barrier((near, rest))
        far = lax.ppermute(near, "band", swap)

        rows = planes * vectors
        flat = (rows, waves // LANES, LANES)
        sent = pack(residual.reshape(flat), local_field.reshape(flat), n_pw)
        got = lax.all_to_all(sent, "pw", split_axis=0, concat_axis=0, tiled=True)

        shape = (planes, span, width)
        psi, h = rotate(
            band, keepers, lattice, got, (chip, rest, near, far), orbital.reshape(shape), energy.reshape(shape)
        )
        return psi.reshape(orbital.shape), h.reshape(energy.shape)

    in_specs = (
        P(None, "pw", "band", None),
        P(None, "pw", "band", None),
        P(None, None, "band", "pw"),
        P(None, None, "band", "pw"),
        P("band", None, None),
        P(),
        P("band", "pw"),
    )
    out_specs = (P(None, None, "band", "pw"), P(None, None, "band", "pw"))
    return jax.shard_map(
        per_device, mesh=mesh, in_specs=in_specs, out_specs=out_specs, check_vma=False
    )
```
